128 devices in a mesh: grp: 4 (over z), dev: 32 (over y, x, core).
Axes of the slice: x: 4, y: 4, z: 4, core: 2. Of those that a mesh axis runs over, the one named last changes fastest.
Arguments:
- adjoint_load: float32 [4096, 64, 128], P(('grp', 'dev')), as said below
- local_ops: float32 [4, 8064, 64, 64], P(None, ('grp', 'dev')), as said below
- coarse_ops: float32 [4, 4, 28, 64, 64], P(None, 'grp'), as said below
- slab_order: int32 [128, 32], P(('grp', 'dev')), may hold values from 0 to 31, each once within a row
Outputs:
- slab_adjoint: float32 [4096, 64, 128], P(('grp', 'dev'))
The draws below stay inside these ranges and needn't reach their ends.
Inputs may be any that keep to these rules, and one draw needn't show every extreme that they name: `local_ops`: blocks of kind 3 approximate the inverses of the diagonal blocks. `coarse_ops`: same four kinds of blocks as local_ops. `adjoint_load`: real-valued right-hand sides. `slab_order`: each row lists every one of the 32 rows of one device once.
All inputs are finite; a program needn't handle non-finite values.
Results may differ from the reference program's by a relative error of at most 0.0001.
Values sent between devices are 32-bit elements; how exact they have to be, the bound alone decides.
No kernel may reach another device: no remote copies, remote signals or barrier semaphores. Data moves between devices by JAX's collectives and lax.ppermute only.
A program may use at most 64 MiB of HBM per device.

```python
import math
import jax
import jax.numpy as jnp
from jax import lax

B = 64
K = 128
R0 = 32
AGG = 3
GROUPS = 4
GROUP_ROWS = 1024
FINE_ROWS = 4096
OPS_ROWS = 8064
CROWS = 28


def make_blocks(key, leading):
    keys = jax.random.split(key, 6)
    shape = leading + (B, B)
    identity = (lax.broadcasted_iota(jnp.int32, (B, B), 0) == lax.broadcasted_iota(jnp.int32, (B, B), 1)).astype(jnp.float32)
    noise = 0.03 * jax.random.normal(keys[0], shape, jnp.float32)
    dscale = jnp.exp(jax.random.uniform(keys[1], leading + (1, 1), jnp.float32, math.log(2.0), math.log(5.0)))
    lower_frac = jax.random.uniform(keys[2], leading + (1, 1), jnp.float32, 0.4, 0.48)
    upper_frac = jax.random.uniform(keys[3], leading + (1, 1), jnp.float32, 0.4, 0.48)
    lower_noise = 0.02 * jax.random.normal(keys[4], shape, jnp.float32)
    upper_noise = 0.02 * jax.random.normal(keys[5], shape, jnp.float32)
    lower = -dscale * lower_frac * (identity + lower_noise)
    upper = -dscale * upper_frac * (identity + upper_noise)
    diagonal = dscale * (identity + noise)
    inverse = (identity - noise) / dscale
    return jnp.stack([lower, diagonal, upper, inverse])


def draw_local_ops(key, part):
    return make_blocks(key, (OPS_ROWS,))


def draw_coarse_ops(key, part):
    return make_blocks(jax.random.fold_in(key, 7), (GROUPS, CROWS))


def draw_adjoint_load(key, part):
    base = jax.random.normal(key, (FINE_ROWS, B, K), jnp.float32)
    return base + 0.5


def setup_inputs(seed: int = 0) -> dict:
    arg_keys = jax.random.split(jax.random.key(seed), 5)
    return {
        "adjoint_load": draw_adjoint_load(jax.random.fold_in(arg_keys[4], 71), 0),
        "local_ops": draw_local_ops(jax.random.fold_in(arg_keys[4], 71), 0),
        "coarse_ops": draw_coarse_ops(jax.random.fold_in(arg_keys[4], 71), 0),
        "slab_order": jax.vmap(lambda own: jax.random.permutation(own, R0))(jax.random.split(arg_keys[3], (FINE_ROWS // R0))).reshape((FINE_ROWS // R0, R0)).astype(jnp.int32),
    }


damping = 0.8


def block_apply(blocks, values):
    return jnp.einsum("rij,rjk->rik", blocks, values, precision=lax.Precision.HIGHEST)


def operate(blocks, values):
    border = jnp.zeros((1,) + values.shape[1:], values.dtype)
    before = jnp.concatenate([border, values[:-1]], axis=0)
    following = jnp.concatenate([values[1:], border], axis=0)
    return (block_apply(blocks[0], before) + block_apply(blocks[1], values)) + block_apply(blocks[2], following)


def halve_rows(residual):
    paired = residual.reshape((residual.shape[0] // 2, 2) + residual.shape[1:])
    return 0.5 * (paired[:, 0] + paired[:, 1])


def vcycle(levels, section_id, source):
    blocks = levels[section_id]
    solution = damping * block_apply(blocks[3], source)
    if section_id + 1 < len(levels):
        residual = source - operate(blocks, solution)
        correction = vcycle(levels, section_id + 1, halve_rows(residual))
        solution = solution + jnp.repeat(correction, 2, axis=0)
    solution = solution + damping * block_apply(blocks[3], source - operate(blocks, solution))
    return solution


def reference(adjoint_load, local_ops, coarse_ops, slab_order):
    local_levels = R0.bit_length()
    devices = GROUP_ROWS // R0
    per_device = 2 * R0 - 1
    results = []
    for group_id in range(GROUPS):
        blocks_all = local_ops[:, group_id * devices * per_device:(group_id + 1) * devices * per_device]
        blocks_all = blocks_all.reshape(4, devices, per_device, B, B)
        levels = []
        offset = 0
        for level_id in range(local_levels):
            height = R0 >> level_id
            shaped = blocks_all[:, :, offset:offset + height]
            levels.append(shaped.reshape(4, devices * height, B, B))
            offset += height
        for section_id in range(1, AGG + 1):
            begin_row = devices - devices // 2 ** (section_id - 1)
            levels.append(coarse_ops[:, group_id, begin_row:begin_row + devices // 2 ** section_id])
        source = adjoint_load[group_id * GROUP_ROWS:(group_id + 1) * GROUP_ROWS]
        initial = vcycle(levels, 0, source)
        residual = source - operate(levels[0], initial)
        results.append(initial + vcycle(levels, 0, residual))
    stacked = jnp.stack(results).reshape(GROUPS, devices, R0, B, K)
    ordering = slab_order.reshape(GROUPS, devices, R0)
    permuted = jax.vmap(jax.vmap(lambda values, picks: values[picks]))(stacked, ordering)
    pieces = permuted.reshape(GROUPS, devices, GROUPS, R0 // GROUPS, B, K)
    return jnp.transpose(pieces, (2, 1, 0, 3, 4, 5)).reshape(FINE_ROWS, B, K)
```

```python
import functools

import jax
import jax.numpy as jnp
from jax import lax
from jax.experimental import pallas as pl
from jax.experimental.pallas import tpu as pltpu
from jax.sharding import PartitionSpec as P

F32, BF16 = jnp.float32, jnp.bfloat16
DAMPING = 0.8
B, K = 64, 128
FINE = (32, 16, 8)
HALO = (11, 5, 2)
HALO_AT = (0, 11, 16)
HALO_ALL = 18
OWN_AT = (0, 32, 48)
CHIP = (4, 2, 1)
COARSE = (16, 8, 4)
COARSE_AT = (0, 16, 24)


def split_pair(pair, first_ref, second_ref):
    lane = lax.broadcasted_iota(jnp.int32, pair.shape, 1)
    high = pair.astype(BF16).astype(F32)
    low = pair - high
    left = lane < 64
    first_ref[...] = jnp.where(left, high, pltpu.roll(low, 64, 1)).astype(BF16)
    second_ref[...] = jnp.where(left, pltpu.roll(high, 64, 1), low).astype(BF16)


def split_row(smooth_lower, diag_upper, row_ref):
    lane = lax.broadcasted_iota(jnp.int32, smooth_lower.shape, 1)
    smooth_lower = jnp.where(lane < 64, smooth_lower * DAMPING, smooth_lower)
    split_pair(smooth_lower, row_ref.at[0:64], row_ref.at[64:128])
    split_pair(diag_upper, row_ref.at[128:192], row_ref.at[192:256])


def stack_rhs(value):
    high = value.astype(BF16)
    low = (value - high.astype(F32)).astype(BF16)
    return jnp.concatenate([high, high, low, low], axis=0)


def product(blocks, value):
    return jnp.dot(
        jnp.concatenate([blocks, blocks], axis=1), stack_rhs(value), preferred_element_type=F32
    )


def grouped(start, stop, size, body, carry=()):
    groups = (stop - start) // size
    if groups > 1:
        carry = lax.fori_loop(
            0, groups, lambda g, held: body(start + g * size, size, held), carry
        )
        start += groups * size
    while start < stop:
        count = min(size, stop - start)
        carry = body(start, count, carry)
        start += count
    return carry


def smooth(rows, q_ref, q_at, source, store, size=6):
    def body(first, count, carry):
        values = [source(first + u) for u in range(count)]
        outs = [product(q_ref[q_at + first + u, 0:64, :], values[u]) for u in range(count)]
        for u in range(count):
            store(first + u, outs[u])
        return carry

    grouped(0, rows, size, body)


def sweep(rows, q_ref, q_at, source, emit, size=4):
    def lower(k):
        return q_ref[q_at + k, 64:128, :]

    def diag(k):
        return q_ref[q_at + k, 128:192, :]

    def upper(k):
        return q_ref[q_at + k, 192:256, :]

    below = product(lower(1), source(0))
    out = product(jnp.concatenate([diag(1), lower(2)], axis=0), source(1))
    carry = (below + out[0:64], out[64:128])

    def body(first, count, carry):
        total, below = carry
        values = [source(first + u) for u in range(count)]
        outs = []
        for u in range(count):
            k = first + u
            blocks = jnp.concatenate([upper(k - 1), diag(k), lower(k + 1)], axis=0)
            outs.append(product(blocks, values[u]))
        for u in range(count):
            emit(first + u - 1, total + outs[u][0:64])
            total = outs[u][64:128] + below
            below = outs[u][128:192]
        return total, below

    total, below = grouped(2, rows - 1, size, body, carry)
    emit(rows - 2, total + product(upper(rows - 2), source(rows - 1)))


class Copies:
    def __init__(self, sems):
        self.sems, self.used = sems, 0

    def start(self, source, target):
        copy = pltpu.make_async_copy(source, target, self.sems.at[self.used])
        copy.start()
        self.used += 1
        return copy


def wait_all(copies):
    for copy in copies:
        copy.wait()


ANY = pl.BlockSpec(memory_space=pl.ANY)
SMEM = pl.BlockSpec(memory_space=pltpu.SMEM)
VMEM = pl.BlockSpec(memory_space=pltpu.VMEM)


def shape(*dims, dtype=F32):
    return jax.ShapeDtypeStruct(dims, dtype)


def call(kernel, name, in_specs, out_specs, out_shape, scratch=(), flops=0, size=0):
    return pl.pallas_call(
        kernel,
        name=name,
        in_specs=in_specs,
        out_specs=out_specs,
        out_shape=out_shape,
        scratch_shapes=list(scratch),
        cost_estimate=pl.CostEstimate(flops=flops, bytes_accessed=size, transcendentals=0),
    )


def rows_of(count):
    return pltpu.VMEM((count, B, K), F32)


def blocks_of(count):
    return pltpu.VMEM((count, 256, 128), BF16)


def send_kernel(info, ops, load, to_in, to_out, own, buf, edge, sems):
    parity = info[0]
    copies = Copies(sems)
    started = []
    for level in range(3):
        rows, halo, at = FINE[level], HALO[level], HALO_AT[level]
        for side, last in ((0, 1 - parity), (1, parity)):
            begin = OWN_AT[level] + (rows - halo) * last
            target = buf.at[:, pl.ds(side * HALO_ALL + at, halo)]
            started.append(copies.start(ops.at[:, pl.ds(begin, halo)], target))
    started.append(copies.start(ops.at[:, pl.ds(56, 7)], buf.at[:, pl.ds(2 * HALO_ALL, 7)]))
    loads = []
    for side, last in ((0, 1 - parity), (1, parity)):
        begin = (FINE[0] - HALO[0]) * last
        loads.append(copies.start(load.at[pl.ds(begin, HALO[0])], edge.at[side]))
    wait_all(started)

    def pack(i, target, at):
        target[at] = jnp.concatenate([buf[3, i], buf[0, i]], axis=1)
        target[at + 1] = jnp.concatenate([buf[1, i], buf[2, i]], axis=1)

    def halo_row(i, carry):
        pack(i, to_in, 2 * i)
        pack(i + HALO_ALL, to_out, 2 * i)
        return carry

    lax.fori_loop(0, HALO_ALL, halo_row, 0)

    def own_row(i, carry):
        pack(i + 2 * HALO_ALL, own, 2 * i)
        return carry

    lax.fori_loop(0, 7, own_row, 0)
    wait_all(loads)
    to_in[pl.ds(2 * HALO_ALL, HALO[0])] = edge[0]
    to_out[pl.ds(2 * HALO_ALL, HALO[0])] = edge[1]


def own_kernel(ops, coarse, q_own, q_coarse, buf, cbuf, q_buf, qc_buf, sems):
    copies = Copies(sems)
    loads = [copies.start(ops.at[:, pl.ds(14 * s, 14)], buf.at[:, pl.ds(14 * s, 14)]) for s in range(4)]
    loads.append(copies.start(coarse.at[:, 0], cbuf))
    stores = []

    def pack(source, i, target):
        split_row(
            jnp.concatenate([source[3, i], source[0, i]], axis=1),
            jnp.concatenate([source[1, i], source[2, i]], axis=1),
            target.at[i],
        )

    for s in range(4):
        loads[s].wait()

        def row(i, carry):
            pack(buf, 14 * s + 2 * i, q_buf)
            pack(buf, 14 * s + 2 * i + 1, q_buf)
            return carry

        lax.fori_loop(0, 7, row, 0)
        stores.append(copies.start(q_buf.at[pl.ds(14 * s, 14)], q_own.at[pl.ds(14 * s, 14)]))
    loads[4].wait()

    def coarse_row(i, carry):
        pack(cbuf, 2 * i, qc_buf)
        pack(cbuf, 2 * i + 1, qc_buf)
        return carry

    lax.fori_loop(0, 14, coarse_row, 0)
    stores.append(copies.start(qc_buf, q_coarse))
    wait_all(stores)


def halo_kernel(got_in, got_out, q_in, q_out):
    def row(i, carry):
        split_row(got_in[2 * i], got_in[2 * i + 1], q_in.at[i])
        split_row(got_out[2 * i], got_out[2 * i + 1], q_out.at[i])
        return carry

    lax.fori_loop(0, HALO_ALL, row, 0)


CHIP_AT = (0, 4, 6)
CHIPQ_AT = (0, 24, 36)
CHIPQ_ROWS = 42


def chip_slots(parity):
    return (
        (0, 0, 2 + parity),
        (1, 0, 3 - parity),
        (2, 0, 1 + 3 * parity),
        (2, 1, 5 * parity),
        (3, 0, 4 - 3 * parity),
        (3, 1, 5 - 5 * parity),
    )


def chip_kernel(info, own, partner, mine, theirs, q_chip):
    arrays = (own, partner, mine, theirs)
    for which, offset, slot in chip_slots(info[0]):
        for level in range(3):
            rows = CHIP[level]
            for i in range(rows):
                at = 2 * (7 * offset + CHIP_AT[level] + i)
                split_row(
                    arrays[which][at],
                    arrays[which][at + 1],
                    q_chip.at[CHIPQ_AT[level] + slot * rows + i],
                )


def down_kernel(
    at, info, load, load_in, load_out, q_own, q_in, q_out, b3, x0_out, x1_out, b1_out, x2_out, b2_out,
    q0, q1, q2, b0, x0, r, b1, x1, b2, x2, sems,
):
    parity = info[0]
    copies = Copies(sems)
    rows, halo = FINE[0], HALO[0]
    left_right = ((load_in, q_in, 1 - parity), (load_out, q_out, parity))
    first = [
        copies.start(load, b0.at[pl.ds(halo, rows)]),
        copies.start(q_own.at[pl.ds(0, rows)], q0.at[pl.ds(halo, rows)]),
    ]
    for values, blocks, right in left_right:
        begin = (rows + halo) * right
        first.append(copies.start(values.at[pl.ds(at, halo)], b0.at[pl.ds(begin, halo)]))
        first.append(copies.start(blocks.at[pl.ds(0, halo)], q0.at[pl.ds(begin, halo)]))
    later = []
    for level, target in ((1, q1), (2, q2)):
        rows, halo = FINE[level], HALO[level]
        group = [copies.start(q_own.at[pl.ds(OWN_AT[level], rows)], target.at[pl.ds(halo, rows)])]
        for _, blocks, right in left_right:
            begin = (rows + halo) * right
            source = blocks.at[pl.ds(HALO_AT[level], halo)]
            group.append(copies.start(source, target.at[pl.ds(begin, halo)]))
        later.append(group)
    wait_all(first)
    stores = []

    def level_down(rows, q, b, x, source):
        def keep(i, value):
            x[i] = value

        smooth(rows, q, 0, source, keep)

        def emit(k, value):
            r[k - 1] = b[k] - value

        return emit

    def read0(i):
        return b0[i]

    emit = level_down(54, q0, b0, x0, read0)
    stores.append(copies.start(x0.at[pl.ds(9, 36)], x0_out))
    sweep(54, q0, 0, lambda k: x0[k], emit)

    def restrict(target, rows, shift):
        def body(first, count, carry):
            for u in range(count):
                i = first + u
                target[i] = 0.5 * (r[2 * i + shift] + r[2 * i + shift + 1])
            return carry

        grouped(0, rows, 4, body)

    restrict(b1, 26, 0)
    wait_all(later[0])
    emit = level_down(26, q1, b1, x1, lambda i: b1[i])
    stores.append(copies.start(x1.at[pl.ds(3, 20)], x1_out))
    stores.append(copies.start(b1.at[pl.ds(4, 18)], b1_out))
    sweep(26, q1, 0, lambda k: x1[k], emit)
    restrict(b2, 12, 0)
    wait_all(later[1])
    emit = level_down(12, q2, b2, x2, lambda i: b2[i])
    stores.append(copies.start(x2, x2_out))
    stores.append(copies.start(b2.at[pl.ds(1, 10)], b2_out))
    sweep(12, q2, 0, lambda k: x2[k], emit)
    for i in range(4):
        b3[i] = 0.5 * (r[2 * i + 1] + r[2 * i + 2])
    wait_all(stores)


def chip_down_kernel(
    info, own, partner, mine, theirs, q_chip, c6, x5_send, x3, b3, x4, b4, x5, b5, q, b_all, r, sems
):
    parity = info[0]
    copies = Copies(sems)
    arrays = (own, partner, mine, theirs)
    first = [copies.start(q_chip.at[pl.ds(0, 24)], q.at[pl.ds(0, 24)])]
    later = copies.start(q_chip.at[pl.ds(24, 18)], q.at[pl.ds(24, 18)])
    for which, offset, slot in chip_slots(parity):
        source = arrays[which].at[pl.ds(4 * offset, 4)]
        first.append(copies.start(source, b_all.at[pl.ds(4 * slot, 4)]))
    wait_all(first)

    def level_down(rows, q_at, b, x):
        def keep(i, value):
            x[i] = value

        smooth(rows, q, q_at, lambda i: b[i], keep)

        def emit(k, value):
            r[k - 1] = b[k] - value

        sweep(rows, q, q_at, lambda k: x[k], emit)

    def copy_row(i, carry):
        b3[i] = b_all[i + 1]
        return carry

    lax.fori_loop(0, 22, copy_row, 0)
    level_down(22, 1, b3, x3)
    for i in range(10):
        b4[i] = 0.5 * (r[2 * i] + r[2 * i + 1])
    later.wait()
    level_down(10, CHIPQ_AT[1] + 1, b4, x4)
    for i in range(4):
        b5[i] = 0.5 * (r[2 * i] + r[2 * i + 1])
    level_down(4, CHIPQ_AT[2] + 1, b5, x5)
    c6[0] = 0.5 * (r[0] + r[1])
    x5_send[0] = x5[1 + parity]


def up_kernel(last, at, *refs):
    refs = list(refs)

    def take(count):
        taken = refs[:count]
        del refs[:count]
        return taken

    (info,) = take(1)
    order = take(1)[0] if last else None
    gathered = take(4)
    x5, b5, x5_got, x4, b4, x3, b3 = take(7)
    x2, b2, x1, b1, x0, load, load_in, load_out = take(8)
    q_coarse, q_chip, q_own, q_in, q_out = take(5)
    earlier = take(1)[0] if last else None
    if last:
        outs = take(4)
    else:
        first_out, load_next, next_in, next_out = take(4)
    (qc, qk, q2, q1, q0, xc, bc, ec7, ec8, xk3, bk3, xk4, bk4, xk5, bk5,
     v2, w2, v1, w1, v0, w0, f, g, xp, r, sums, sems) = refs
    parity, chip, row_y, row_x, group = (info[i] for i in range(5))
    copies = Copies(sems)

    coarse_at = (1, 19, 29)
    waits_coarse = []
    for sy in range(4):
        for sx in range(4):
            place = 4 * lax.rem(row_y + 4 - sy, 4) + lax.rem(row_x + 4 - sx, 4)
            waits_coarse.append(copies.start(gathered[sy].at[sx], bc.at[1 + place]))
    for level in range(3):
        source = q_coarse.at[pl.ds(COARSE_AT[level], COARSE[level])]
        waits_coarse.append(copies.start(source, qc.at[pl.ds(coarse_at[level], COARSE[level])]))
    waits_chip = [
        copies.start(q_chip, qk),
        copies.start(x5, xk5.at[pl.ds(1, 4)]),
        copies.start(b5, bk5),
        copies.start(x4, xk4),
        copies.start(b4, bk4),
        copies.start(x3, xk3),
        copies.start(b3, bk3),
    ]
    waits_fine = []
    for level, q, values, saved, right_side, saved_b in (
        (2, q2, v2, x2, w2, b2), (1, q1, v1, x1, w1, b1), (0, q0, v0, x0, w0, None),
    ):
        rows, halo = FINE[level], HALO[level]
        group_waits = [
            copies.start(q_own.at[pl.ds(OWN_AT[level], rows)], q.at[pl.ds(2, rows)]),
            copies.start(saved, values),
        ]
        for blocks, right in ((q_in, 1 - parity), (q_out, parity)):
            begin = HALO_AT[level] + (halo - 2) * (1 - right)
            target = q.at[pl.ds((rows + 2) * right, 2)]
            group_waits.append(copies.start(blocks.at[pl.ds(begin, 2)], target))
        if level:
            group_waits.append(copies.start(saved_b, right_side))
        else:
            group_waits.append(copies.start(load, right_side.at[pl.ds(1, rows)]))
            for values_in, right in ((load_in, 1 - parity), (load_out, parity)):
                begin = at + (halo - 1) * (1 - right)
                target = right_side.at[pl.ds((rows + 1) * right, 1)]
                group_waits.append(copies.start(values_in.at[pl.ds(begin, 1)], target))
        waits_fine.append(group_waits)
    if last:
        wait_sums = copies.start(earlier, sums)

    zero = jnp.zeros((B, K), F32)
    for level in range(3):
        for edge in (coarse_at[level] - 1, coarse_at[level] + COARSE[level]):
            xc[edge] = zero
    wait_all(waits_coarse)

    for level in range(3):
        rows, base = COARSE[level], coarse_at[level]

        def keep(i, value):
            xc[base + i] = value

        smooth(rows, qc, base, lambda i: bc[base + i], keep)
        if level == 2:
            break

        def emit(k, value):
            r[k - 1] = bc[base - 1 + k] - value

        sweep(rows + 2, qc, base - 1, lambda k: xc[base - 1 + k], emit)
        following = coarse_at[level + 1]
        for i in range(rows // 2):
            bc[following + i] = 0.5 * (r[2 * i] + r[2 * i + 1])

    for level in (2, 1, 0):
        rows, base = COARSE[level], coarse_at[level]
        if level < 2:
            below = coarse_at[level + 1]
            for i in range(rows):
                xc[base + i] = xc[base + i] + xc[below + i // 2]

        def emit(k, value):
            r[k - 1] = bc[base - 1 + k] - value

        sweep(rows + 2, qc, base - 1, lambda k: xc[base - 1 + k], emit)

        def keep(i, value):
            xc[base + i] = xc[base + i] + value

        smooth(rows, qc, base, lambda i: r[i], keep)

    def post(rows, q, q_at, right_side, b_at, target, size_s=6):
        def emit(k, value):
            r[k - 1] = right_side[b_at + k - 1] - value

        sweep(rows + 4, q, q_at, lambda k: xp[k], emit)

        def keep(i, value):
            target[i] = xp[i + 1] + value

        smooth(rows + 2, q, q_at + 1, lambda i: r[i], keep)

    def correct(rows, values, x_at, source):
        def body(first, count, carry):
            for u in range(count):
                j = first + u
                value = source[j]
                xp[2 * j] = values[x_at + 2 * j] + value
                xp[2 * j + 1] = values[x_at + 2 * j + 1] + value
            return carry

        grouped(0, rows // 2 + 2, 3, body)

    wait_all(waits_chip)
    xk5[5 * parity] = x5_got[0]
    for k in range(5):
        xp[k] = xk5[k + parity] + xc[chip + lax.div(k + parity, 2)]
    post(1, qk, CHIPQ_AT[2] + parity, bk5, parity, f)
    correct(2, xk4, 1 + 2 * parity, f)
    post(2, qk, CHIPQ_AT[1] + 2 + 2 * parity, bk4, 2 + 2 * parity, g)
    correct(4, xk3, 5 + 4 * parity, g)
    post(4, qk, 6 + 4 * parity, bk3, 6 + 4 * parity, f)
    wait_all(waits_fine[0])
    correct(8, v2, 0, f)
    post(8, q2, 0, w2, 0, g)
    wait_all(waits_fine[1])
    correct(16, v1, 0, g)
    post(16, q1, 0, w1, 0, f)
    wait_all(waits_fine[2])
    correct(32, v0, 0, f)
    post(32, q0, 0, w0, 0, g)

    if last:
        wait_sums.wait()
        for s in range(4):
            base = 8 * lax.rem(group + s, 4)
            for u in range(8):
                pick = order[0, base + u]
                outs[s][u] = sums[pick] + g[pick + 1]
        return
    stores = [copies.start(g.at[pl.ds(1, 32)], first_out)]

    def emit(k, value):
        r[k - 1] = w0[k] - value

    sweep(34, q0, 1, lambda k: g[k], emit)
    stores.append(copies.start(r.at[pl.ds(0, 32)], load_next))
    stores.append(copies.start(r.at[pl.ds(21 * (1 - parity), 11)], next_in))
    stores.append(copies.start(r.at[pl.ds(21 * parity, 11)], next_out))
    wait_all(stores)


def place_kernel(info, part0, part1, part2, part3, out, sems):
    copies = Copies(sems)
    started = []
    for s, part in enumerate((part0, part1, part2, part3)):
        begin = 8 * lax.rem(info[4] + 4 - s, 4)
        started.append(copies.start(part, out.at[pl.ds(begin, 8)]))
    wait_all(started)


def shards(adjoint_load, local_ops, coarse_ops, slab_order):
    devices = lax.axis_size("dev")
    position = lax.axis_index("dev")
    chips = devices // 2
    side = 4
    chip = position // 2
    info = jnp.stack(
        [position % 2, chip, chip // side, chip % side, lax.axis_index("grp")]
    ).astype(jnp.int32)

    def swap_in(value):
        return lax.ppermute(value, "dev", [(i, i ^ 1) for i in range(devices)])

    def swap_out(value):
        route = []
        for i in range(1, devices - 1, 2):
            route += [(i, i + 1), (i + 1, i)]
        return lax.ppermute(value, "dev", route)

    def around(value):
        partner = swap_in(value)
        mine = swap_out(jnp.concatenate([value, partner], axis=0))
        theirs = swap_in(mine)
        return value, partner, mine, theirs

    def next_but_one(value):
        route = []
        for i in range(devices):
            other = i + 2 if i % 2 == 0 else i - 2
            if 0 <= other < devices:
                route.append((i, other))
        return lax.ppermute(value, "dev", route)

    def shift(value, along_y, step):
        route = []
        for i in range(devices):
            y, x, core = i // (2 * side), i // 2 % side, i % 2
            if along_y:
                y = (y + step) % side
            else:
                x = (x + step) % side
            route.append((i, (y * side + x) * 2 + core))
        return lax.ppermute(value, "dev", route)

    def gather(value):
        row = jnp.concatenate([value] + [shift(value, False, s) for s in (1, 2, 3)], axis=0)
        return [row] + [shift(row, True, s) for s in (1, 2, 3)]

    halo_rows = 2 * HALO_ALL + HALO[0]
    to_in, to_out, own7 = call(
        send_kernel, "send",
        [SMEM, ANY, ANY], [VMEM] * 3,
        [shape(halo_rows, B, K)] * 2 + [shape(14, B, K)],
        [pltpu.VMEM((4, 43, B, B), F32), pltpu.VMEM((2, HALO[0], B, K), F32), pltpu.SemaphoreType.DMA((9,))],
        size=12 << 20,
    )(info, local_ops, adjoint_load)
    got_in, got_out = swap_in(to_in), swap_out(to_out)
    q_own, q_coarse = call(
        own_kernel, "own",
        [ANY, ANY], [ANY] * 2,
        [shape(56, 256, 128, dtype=BF16), shape(28, 256, 128, dtype=BF16)],
        [pltpu.VMEM((4, 56, B, B), F32), pltpu.VMEM((4, 28, B, B), F32), blocks_of(56), blocks_of(28),
         pltpu.SemaphoreType.DMA((10,))],
        size=16 << 20,
    )(local_ops, coarse_ops)
    q_in, q_out = call(
        halo_kernel, "halo",
        [VMEM] * 2, [VMEM] * 2, [shape(HALO_ALL, 256, 128, dtype=BF16)] * 2,
        size=6 << 20,
    )(got_in, got_out)
    q_chip = call(
        chip_kernel, "chip",
        [SMEM] + [VMEM] * 4, VMEM, shape(CHIPQ_ROWS, 256, 128, dtype=BF16),
        size=6 << 20,
    )(info, *around(own7))

    def down(at, load, load_in, load_out):
        return call(
            functools.partial(down_kernel, at), "down",
            [SMEM] + [ANY] * 6, [VMEM] + [ANY] * 5,
            [shape(4, B, K), shape(36, B, K), shape(20, B, K), shape(18, B, K), shape(12, B, K), shape(10, B, K)],
            [blocks_of(54), blocks_of(26), blocks_of(12), rows_of(54), rows_of(54), rows_of(52),
             rows_of(26), rows_of(26), rows_of(12), rows_of(12), pltpu.SemaphoreType.DMA((17,))],
            flops=92 * 4 * 2 * 64 * 256 * 128, size=16 << 20,
        )(info, load, load_in, load_out, q_own, q_in, q_out)

    def chip_down(b3):
        return call(
            chip_down_kernel, "chip_down",
            [SMEM] + [ANY] * 5, [VMEM] * 8,
            [shape(1, B, K), shape(1, B, K), shape(22, B, K), shape(22, B, K), shape(10, B, K), shape(10, B, K),
             shape(4, B, K), shape(4, B, K)],
            [blocks_of(CHIPQ_ROWS), rows_of(24), rows_of(20), pltpu.SemaphoreType.DMA((8,))],
            flops=36 * 4 * 2 * 64 * 256 * 128, size=6 << 20,
        )(info, *around(b3), q_chip)

    def cycle(at, load, load_in, load_out, earlier=None):
        last = earlier is not None
        b3, x0, x1, b1, x2, b2 = down(at, load, load_in, load_out)
        c6, x5_send, x3, b3c, x4, b4, x5, b5 = chip_down(b3)
        gathered = gather(c6)
        x5_got = next_but_one(x5_send)
        operands = [info] + ([slab_order] if last else []) + gathered
        operands += [x5, b5, x5_got, x4, b4, x3, b3c, x2, b2, x1, b1, x0, load, load_in, load_out]
        operands += [q_coarse, q_chip, q_own, q_in, q_out] + ([earlier] if last else [])
        specs = [SMEM] + ([SMEM] if last else []) + [ANY] * 4 + [ANY, ANY, VMEM] + [ANY] * 4
        specs += [ANY] * 8 + [ANY] * 5 + ([ANY] if last else [])
        if last:
            out_shape, out_specs = [shape(8, B, K)] * 4, [VMEM] * 4
        else:
            out_shape = [shape(32, B, K)] * 2 + [shape(11, B, K)] * 2
            out_specs = [ANY] * 4
        return call(
            functools.partial(up_kernel, last, at), "up",
            specs, out_specs, out_shape,
            [blocks_of(34), blocks_of(CHIPQ_ROWS), blocks_of(12), blocks_of(20), blocks_of(36),
             rows_of(34), rows_of(34), rows_of(1), rows_of(1),
             rows_of(22), rows_of(22), rows_of(10), rows_of(10), rows_of(6), rows_of(4),
             rows_of(12), rows_of(10), rows_of(20), rows_of(18), rows_of(36), rows_of(34),
             rows_of(34), rows_of(34), rows_of(36), rows_of(34), rows_of(32),
             pltpu.SemaphoreType.DMA((48,))],
            flops=130 * 4 * 2 * 64 * 256 * 128, size=20 << 20,
        )(*operands)

    first, load_next, next_in, next_out = cycle(2 * HALO_ALL, adjoint_load, got_in, got_out)
    parts = cycle(0, load_next, swap_in(next_in), swap_out(next_out), first)

    groups = lax.axis_size("grp")
    arrived = [parts[0]]
    for s in range(1, groups):
        arrived.append(lax.ppermute(parts[s], "grp", [(i, (i + s) % groups) for i in range(groups)]))
    return call(
        place_kernel, "place",
        [SMEM] + [VMEM] * 4, ANY, shape(32, B, K),
        [pltpu.SemaphoreType.DMA((4,))], size=2 << 20,
    )(info, *arrived)


def solution(mesh):
    placed = (
        P(("grp", "dev"), None, None),
        P(None, ("grp", "dev"), None, None),
        P(None, "grp", None, None, None),
        P(("grp", "dev"), None),
    )
    return jax.shard_map(
        shards, mesh=mesh, in_specs=placed, out_specs=P(("grp", "dev"), None, None), check_vma=False
    )
```

```python
import functools

import jax
import jax.numpy as jnp
from jax import lax
from jax.experimental import pallas as pl
from jax.experimental.pallas import tpu as pltpu
from jax.sharding import PartitionSpec as P


F32, BF16 = jnp.float32, jnp.bfloat16
DAMPING = 0.8
B, K = 64, 128
FINE = (32, 16, 8)
HALO = (11, 5, 2)
OWN_AT = (0, 32, 48)
CHIP = (4, 2, 1)
COARSE = (16, 8, 4)
COARSE_AT = (0, 16, 24)


def split_pair(pair, first_ref, second_ref):
    lane = lax.broadcasted_iota(jnp.int32, pair.shape, 1)
    high = pair.astype(BF16).astype(F32)
    low = pair - high
    left = lane < 64
    first_ref[...] = jnp.where(left, high, pltpu.roll(low, 64, 1)).astype(BF16)
    second_ref[...] = jnp.where(left, pltpu.roll(high, 64, 1), low).astype(BF16)


def split_row(smooth_lower, diag_upper, row_ref):
    lane = lax.broadcasted_iota(jnp.int32, smooth_lower.shape, 1)
    smooth_lower = jnp.where(lane < 64, smooth_lower * DAMPING, smooth_lower)
    split_pair(smooth_lower, row_ref.at[0:64], row_ref.at[64:128])
    split_pair(diag_upper, row_ref.at[128:192], row_ref.at[192:256])


def stack_rhs(value):
    high = value.astype(BF16)
    low = (value - high.astype(F32)).astype(BF16)
    return jnp.concatenate([high, high, low, low], axis=0)


def product(blocks, value):
    return jnp.dot(
        jnp.concatenate([blocks, blocks], axis=1), stack_rhs(value), preferred_element_type=F32
    )


def grouped(start, stop, size, body, carry=()):
    groups = (stop - start) // size
    if groups > 1:
        carry = lax.fori_loop(
            0, groups, lambda g, held: body(start + g * size, size, held), carry
        )
        start += groups * size
    while start < stop:
        count = min(size, stop - start)
        carry = body(start, count, carry)
        start += count
    return carry


def smooth(rows, q_ref, q_at, source, store, size=12):
    def body(first, count, carry):
        values = [source(first + u) for u in range(count)]
        outs = [product(q_ref[q_at + first + u, 0:64, :], values[u]) for u in range(count)]
        for u in range(count):
            store(first + u, outs[u], values[u])
        return carry

    grouped(0, rows, size, body)


def sweep(rows, q_ref, q_at, source, emit, size=13):
    def lower(k):
        return q_ref[q_at + k, 64:128, :]

    def diag(k):
        return q_ref[q_at + k, 128:192, :]

    def upper(k):
        return q_ref[q_at + k, 192:256, :]

    below = product(lower(1), source(0))
    out = product(jnp.concatenate([diag(1), lower(2)], axis=0), source(1))
    carry = (below + out[0:64], out[64:128])

    def body(first, count, carry):
        total, below = carry
        values = [source(first + u) for u in range(count)]
        outs = []
        for u in range(count):
            k = first + u
            blocks = jnp.concatenate([upper(k - 1), diag(k), lower(k + 1)], axis=0)
            outs.append(product(blocks, values[u]))
        for u in range(count):
            emit(first + u - 1, total + outs[u][0:64])
            total = outs[u][64:128] + below
            below = outs[u][128:192]
        return total, below

    total, below = grouped(2, rows - 1, size, body, carry)
    emit(rows - 2, total + product(upper(rows - 2), source(rows - 1)))


class Copies:
    def __init__(self, sems):
        self.sems, self.used = sems, 0

    def start(self, source, target):
        copy = pltpu.make_async_copy(source, target, self.sems.at[self.used])
        copy.start()
        self.used += 1
        return copy


def wait_all(copies):
    for copy in copies:
        copy.wait()


ANY = pl.BlockSpec(memory_space=pl.ANY)
SMEM = pl.BlockSpec(memory_space=pltpu.SMEM)
VMEM = pl.BlockSpec(memory_space=pltpu.VMEM)


def shape(*dims, dtype=F32):
    return jax.ShapeDtypeStruct(dims, dtype)


def split_shape(rows):
    return shape(rows, 256, 128, dtype=BF16)


def call(kernel, in_specs, out_shape, scratch=(), flops=0, size=0, room=4, aliases=None):
    return pl.pallas_call(
        kernel,
        in_specs=in_specs,
        out_specs=jax.tree.map(lambda _: VMEM, out_shape),
        out_shape=out_shape,
        scratch_shapes=list(scratch),
        input_output_aliases=aliases or {},
        cost_estimate=pl.CostEstimate(flops=flops, bytes_accessed=size, transcendentals=0),
        compiler_params=pltpu.CompilerParams(vmem_limit_bytes=room << 20),
    )


def rows_of(count):
    return pltpu.VMEM((count, B, K), F32)


def device_parity():
    return lax.rem(lax.axis_index("dev"), 2)


def pack_row(buf, i, target, at):
    target[at] = jnp.concatenate([buf[3, i], buf[0, i]], axis=1)
    target[at + 1] = jnp.concatenate([buf[1, i], buf[2, i]], axis=1)


def send_kernel(outward, ops, load, sent, buf, sems):
    parity = device_parity()
    last = parity if outward else 1 - parity
    copies = Copies(sems)
    halo = HALO[0]
    begin = (FINE[0] - halo) * last
    half = halo // 2
    first = copies.start(ops.at[:, pl.ds(begin, half)], buf.at[:, pl.ds(0, half)])
    second = copies.start(
        ops.at[:, pl.ds(begin + half, halo - half)], buf.at[:, pl.ds(half, halo - half)]
    )
    values = copies.start(load.at[pl.ds(begin, halo)], sent.at[pl.ds(2 * halo, halo)])
    first.wait()
    for i in range(halo):
        if i == half:
            second.wait()
        pack_row(buf, i, sent, 2 * i)
    values.wait()


def send_rest_kernel(ops, to_in, to_out, own, buf, sems):
    parity = device_parity()
    copies = Copies(sems)
    started = []
    for level, at in ((1, 0), (2, 5)):
        rows, halo = FINE[level], HALO[level]
        for side, last in ((0, 1 - parity), (1, parity)):
            begin = OWN_AT[level] + (rows - halo) * last
            target = buf.at[:, pl.ds(7 * side + at, halo)]
            started.append(copies.start(ops.at[:, pl.ds(begin, halo)], target))
    started.append(copies.start(ops.at[:, pl.ds(56, 7)], buf.at[:, pl.ds(14, 7)]))
    wait_all(started)

    def row(i, carry):
        pack_row(buf, i, to_in, 2 * i)
        pack_row(buf, i + 7, to_out, 2 * i)
        pack_row(buf, i + 14, own, 2 * i)
        return carry

    lax.fori_loop(0, 7, row, 0)


COARSE_IN = (1, 19, 29)


def split_rows(source, begin, rows, target, at):
    def pair_of_rows(i, carry):
        for u in range(2):
            k = begin + 2 * i + u
            split_row(
                jnp.concatenate([source[3, k], source[0, k]], axis=1),
                jnp.concatenate([source[1, k], source[2, k]], axis=1),
                target.at[at + 2 * i + u],
            )
        return carry

    lax.fori_loop(0, rows // 2, pair_of_rows, 0)


def own_kernel(ops, q0, buf, sems):
    copies = Copies(sems)
    parts = []
    for begin in (0, 16):
        part = pl.ds(begin, 16)
        parts.append(copies.start(ops.at[:, part], buf.at[:, part]))
    for begin, part in zip((0, 16), parts):
        part.wait()
        split_rows(buf, begin, 16, q0, HALO[0] + begin)


def own_rest_kernel(ops, coarse, q1, q2, qc, buf, cbuf, sems):
    copies = Copies(sems)
    loads = [
        copies.start(ops.at[:, pl.ds(32, 24)], buf),
        copies.start(coarse.at[:, 0], cbuf),
    ]
    loads[0].wait()
    split_rows(buf, 0, 16, q1, HALO[1])
    split_rows(buf, 16, 8, q2, HALO[2])
    loads[1].wait()
    for level in range(3):
        split_rows(cbuf, COARSE_AT[level], COARSE[level], qc, COARSE_IN[level])


def halo_kernel(levels, got_in, got_out, *refs):
    parity = device_parity()
    targets = refs[len(levels):]
    at = 0
    for level, target in zip(levels, targets):
        rows, halo = FINE[level], HALO[level]
        for got, right in ((got_in, 1 - parity), (got_out, parity)):
            begin = (rows + halo) * right

            def row(i, carry):
                split_row(got[2 * (at + i)], got[2 * (at + i) + 1], target.at[begin + i])
                return carry

            lax.fori_loop(0, halo, row, 0)
        at += halo


CHIP_AT = (0, 4, 6)
CHIPQ_AT = (0, 24, 36)
CHIPQ_ROWS = 42


def chip_slots(parity):
    return (
        (0, 0, 2 + parity),
        (1, 0, 3 - parity),
        (2, 0, 1 + 3 * parity),
        (2, 1, 5 * parity),
        (3, 0, 4 - 3 * parity),
        (3, 1, 5 - 5 * parity),
    )


def chip_send_kernel(own, partner, both):
    near = device_parity()

    def own_row(i, carry):
        both[i] = own[i]
        return carry

    lax.fori_loop(0, 14, own_row, 0)
    for i in range(3):
        for u in range(2):
            both[14 + 2 * i + u] = partner[2 * (near + i) + u]
    for u in range(2):
        both[20 + u] = partner[2 * (CHIP_AT[1] + near) + u]


def chip_kernel(own, partner, mine, theirs, q_chip):
    parity = device_parity()
    arrays = (own, partner, mine, theirs)
    for which, offset, slot in chip_slots(parity):
        if offset:
            near = 1 - parity if which == 2 else parity
            moves = [(14 + 2 * i, 4 * slot + near + i) for i in range(3)]
            moves.append((20, CHIPQ_AT[1] + 2 * slot + near))
        else:
            moves = [
                (2 * (CHIP_AT[level] + i), CHIPQ_AT[level] + slot * CHIP[level] + i)
                for level in range(3)
                for i in range(CHIP[level])
            ]
        for at, target in moves:
            split_row(arrays[which][at], arrays[which][at + 1], q_chip.at[target])


def restrict(r, target, rows, shift):
    def body(first, count, carry):
        for u in range(count):
            i = first + u
            target[i] = 0.5 * (r[2 * i + shift] + r[2 * i + shift + 1])
        return carry

    grouped(0, rows, 4, body)


def residual_into(r, b):
    def emit(k, value):
        r[k - 1] = b[k] - value

    return emit


def down_fine_kernel(at, load, load_in, load_out, q0, x0, b0, b1, r):
    parity = device_parity()
    rows, halo = FINE[0], HALO[0]
    for source, shift, count, begin in (
        (load, 0, rows, halo),
        (load_in, at, halo, (rows + halo) * (1 - parity)),
        (load_out, at, halo, (rows + halo) * parity),
    ):

        def keep(i, value, given):
            x0[begin + i] = value
            b0[begin + i] = given

        smooth(count, q0, begin, lambda i: source[shift + i], keep)
    sweep(54, q0, 0, lambda k: x0[k], residual_into(r, b0))
    restrict(r, b1, 26, 0)


def level_down(rows, q, q_at, b, x, r):
    def keep(i, value, given):
        x[i] = value

    smooth(rows, q, q_at, lambda i: b[i], keep)
    sweep(rows, q, q_at, lambda k: x[k], residual_into(r, b))


def down_kernel(b1, q1, q2, x1, x2, b2, b3, r):
    level_down(26, q1, 0, b1, x1, r)
    restrict(r, b2, 12, 0)
    level_down(12, q2, 0, b2, x2, r)
    restrict(r, b3, 4, 1)


def chip_down_kernel(own, partner, mine, theirs, q, c6, c6_x5, x3, b3, x4, b4, x5, b5, r):
    parity = device_parity()
    arrays = (own, partner, mine, theirs)
    for which, offset, slot in chip_slots(parity):
        for i in range(4):
            b3[4 * slot + i] = arrays[which][4 * offset + i]

    def keep(i, value, given):
        x3[i] = value

    smooth(22, q, 1, lambda i: b3[i + 1], keep)

    def emit(k, value):
        r[k - 1] = b3[k + 1] - value

    sweep(22, q, 1, lambda k: x3[k], emit)
    restrict(r, b4, 10, 0)
    level_down(10, q, CHIPQ_AT[1] + 1, b4, x4, r)
    restrict(r, b5, 4, 0)
    level_down(4, q, CHIPQ_AT[2] + 1, b5, x5, r)
    mean = 0.5 * (r[0] + r[1])
    c6[0] = mean
    c6_x5[0] = mean
    c6_x5[1] = x5[1 + parity]


def row_kernel(own, ahead, across, behind, row, row_x5):
    for i, part in enumerate((own, ahead, across, behind)):
        row[i] = part[0]
        row_x5[i] = part[0]

    @pl.when(device_parity() == 0)
    def _():
        row_x5[4] = ahead[1]

    @pl.when(device_parity() == 1)
    def _():
        row_x5[4] = behind[1]


def up_kernel(last, *refs):
    refs = list(refs)

    def take(count):
        taken = refs[:count]
        del refs[:count]
        return taken

    order = take(1)[0] if last else None
    gathered = take(4)
    x5, b5, x4, b4, x3, b3, x2, b2, x1, b1, x0, b0, qc, qk, q2, q1, q0 = take(17)
    sums = take(1)[0] if last else None
    outs = take(4)
    xc, bc, xk5, f, g, xp, r = refs
    position = lax.axis_index("dev")
    parity, chip = lax.rem(position, 2), lax.div(position, 2)
    row_y, row_x = lax.div(chip, 4), lax.rem(chip, 4)

    for sy in range(4):
        for sx in range(4):
            place = 4 * lax.rem(row_y + 4 - sy, 4) + lax.rem(row_x + 4 - sx, 4)
            bc[1 + place] = gathered[sy][sx]
    zero = jnp.zeros((B, K), F32)
    for level in range(3):
        for edge in (COARSE_IN[level] - 1, COARSE_IN[level] + COARSE[level]):
            xc[edge] = zero

    for level in range(3):
        rows, base = COARSE[level], COARSE_IN[level]

        def keep(i, value, given):
            xc[base + i] = value

        smooth(rows, qc, base, lambda i: bc[base + i], keep)
        if level == 2:
            break

        def emit(k, value):
            r[k - 1] = bc[base - 1 + k] - value

        sweep(rows + 2, qc, base - 1, lambda k: xc[base - 1 + k], emit)
        following = COARSE_IN[level + 1]
        for i in range(rows // 2):
            bc[following + i] = 0.5 * (r[2 * i] + r[2 * i + 1])

    for level in (2, 1, 0):
        rows, base = COARSE[level], COARSE_IN[level]
        if level < 2:
            below = COARSE_IN[level + 1]
            for i in range(rows):
                xc[base + i] = xc[base + i] + xc[below + i // 2]

        def emit(k, value):
            r[k - 1] = bc[base - 1 + k] - value

        sweep(rows + 2, qc, base - 1, lambda k: xc[base - 1 + k], emit)

        def keep(i, value, given):
            xc[base + i] = xc[base + i] + value

        smooth(rows, qc, base, lambda i: r[i], keep)

    def post(rows, q, q_at, right_side, b_at, target):
        def emit(k, value):
            r[k - 1] = right_side[b_at + k - 1] - value

        sweep(rows + 4, q, q_at, lambda k: xp[k], emit)

        def keep(i, value, given):
            target[i] = xp[i + 1] + value

        smooth(rows + 2, q, q_at + 1, lambda i: r[i], keep)

    def correct(rows, values, x_at, source):
        def body(first, count, carry):
            for u in range(count):
                j = first + u
                value = source[j]
                xp[2 * j] = values[x_at + 2 * j] + value
                xp[2 * j + 1] = values[x_at + 2 * j + 1] + value
            return carry

        grouped(0, rows // 2 + 2, 3, body)

    for i in range(4):
        xk5[1 + i] = x5[i]
    inside = row_x != 3 * parity
    outermost = chip == 15 * parity

    @pl.when(inside)
    def _():
        xk5[5 * parity] = gathered[0][4]

    @pl.when(jnp.logical_not(inside) & (parity == 0))
    def _():
        xk5[0] = gathered[1][4]

    @pl.when(jnp.logical_not(inside) & (parity == 1))
    def _():
        xk5[5] = gathered[3][4]

    @pl.when(outermost)
    def _():
        xk5[5 * parity] = zero

    for k in range(5):
        xp[k] = xk5[k + parity] + xc[chip + lax.div(k + parity, 2)]
    post(1, qk, CHIPQ_AT[2] + parity, b5, parity, f)
    correct(2, x4, 1 + 2 * parity, f)
    post(2, qk, CHIPQ_AT[1] + 2 + 2 * parity, b4, 2 + 2 * parity, g)
    correct(4, x3, 5 + 4 * parity, g)
    post(4, qk, 6 + 4 * parity, b3, 7 + 4 * parity, f)
    correct(8, x2, 0, f)
    post(8, q2, 0, b2, 1, g)
    correct(16, x1, 3, g)
    post(16, q1, 3, b1, 4, f)
    correct(32, x0, 9, f)
    post(32, q0, 9, b0, 10, g)

    if last:
        group = lax.axis_index("grp")
        for s in range(4):
            base = 8 * lax.rem(group + s, 4)
            for u in range(8):
                pick = order[0, base + u]
                outs[s][u] = sums[pick] + g[pick + 1]
        return
    first_out, load_next, next_in, next_out = outs

    def emit(k, value):
        load_next[k - 1] = b0[k + 10] - value
        first_out[k - 1] = g[k]

    sweep(34, q0, 10, lambda k: g[k], emit)

    def edge_row(i, carry):
        next_in[i] = load_next[21 * (1 - parity) + i]
        next_out[i] = load_next[21 * parity + i]
        return carry

    lax.fori_loop(0, 11, edge_row, 0)


def place_kernel(part0, part1, part2, part3, out, sems):
    copies = Copies(sems)
    started = []
    group = lax.axis_index("grp")
    for s, part in enumerate((part0, part1, part2, part3)):
        begin = 8 * lax.rem(group + 4 - s, 4)
        started.append(copies.start(part, out.at[pl.ds(begin, 8)]))
    wait_all(started)


def shards(adjoint_load, local_ops, coarse_ops, slab_order):
    devices = lax.axis_size("dev")
    side = 4

    def swap_in(value):
        return lax.ppermute(value, "dev", [(i, i ^ 1) for i in range(devices)])

    def swap_out(value):
        route = []
        for i in range(1, devices - 1, 2):
            route += [(i, i + 1), (i + 1, i)]
        return lax.ppermute(value, "dev", route)

    def around(value):
        partner = swap_in(value)
        mine = swap_out(jnp.concatenate([value, partner], axis=0))
        theirs = swap_in(mine)
        return value, partner, mine, theirs

    def shift(value, along_y, step):
        route = []
        for i in range(devices):
            y, x, core = i // (2 * side), i // 2 % side, i % 2
            if along_y:
                y = (y + step) % side
            else:
                x = (x + step) % side
            route.append((i, (y * side + x) * 2 + core))
        return lax.ppermute(value, "dev", route)

    def gather(c6, c6_x5):
        parts = (c6_x5, shift(c6_x5, False, 1), shift(c6, False, 2), shift(c6_x5, False, 3))
        row, row_x5 = call(
            row_kernel, [VMEM] * 4, [shape(4, B, K), shape(5, B, K)], size=1 << 18
        )(*parts)
        return [row_x5, shift(row_x5, True, 1), shift(row, True, 2), shift(row_x5, True, 3)]

    halo = HALO[0]

    def send(outward):
        return call(
            functools.partial(send_kernel, outward), [ANY, ANY], shape(3 * halo, B, K),
            [pltpu.VMEM((4, halo, B, B), F32), pltpu.SemaphoreType.DMA((3,))], size=4 << 20, room=58,
        )(local_ops, adjoint_load)

    got_out = swap_out(send(True))
    got_in = swap_in(send(False))
    rest_in, rest_out, own7 = call(
        send_rest_kernel, [ANY], [shape(14, B, K)] * 3,
        [pltpu.VMEM((4, 21, B, B), F32), pltpu.SemaphoreType.DMA((5,))], size=4 << 20, room=50,
    )(local_ops)
    more_out = swap_out(rest_out)
    more_in = swap_in(rest_in)
    q0 = call(
        own_kernel, [ANY], [split_shape(54)],
        [pltpu.VMEM((4, 32, B, B), F32), pltpu.SemaphoreType.DMA((2,))], size=8 << 20, room=40,
    )(local_ops)[0]
    q1, q2, qc = call(
        own_rest_kernel, [ANY, ANY], [split_shape(26), split_shape(12), split_shape(34)],
        [pltpu.VMEM((4, 24, B, B), F32), pltpu.VMEM((4, 28, B, B), F32), pltpu.SemaphoreType.DMA((2,))],
        size=12 << 20, room=24,
    )(local_ops, coarse_ops)
    q0 = call(
        functools.partial(halo_kernel, (0,)), [VMEM] * 3, [split_shape(54)],
        size=4 << 20, aliases={2: 0},
    )(got_in, got_out, q0)[0]
    q1, q2 = call(
        functools.partial(halo_kernel, (1, 2)), [VMEM] * 4, [split_shape(26), split_shape(12)],
        size=4 << 20, aliases={2: 0, 3: 1},
    )(more_in, more_out, q1, q2)
    partner7 = swap_in(own7)
    both = call(chip_send_kernel, [VMEM] * 2, shape(22, B, K), size=2 << 20)(own7, partner7)
    both = lax.optimization_barrier((both, q0))[0]
    mine = swap_out(both)
    q_chip = call(
        chip_kernel, [VMEM] * 4, split_shape(CHIPQ_ROWS), size=6 << 20,
    )(own7, partner7, mine, swap_in(mine))

    def cycle(at, load, load_in, load_out, earlier=None):
        last = earlier is not None
        x0, b0, b1 = call(
            functools.partial(down_fine_kernel, at),
            [VMEM] * 4, [shape(54, B, K), shape(54, B, K), shape(26, B, K)],
            [rows_of(52)], flops=54 * 4 * 2 * 64 * 256 * 128, size=16 << 20,
        )(load, load_in, load_out, q0)
        x1, x2, b2, b3 = call(
            down_kernel,
            [VMEM] * 3, [shape(26, B, K), shape(12, B, K), shape(12, B, K), shape(4, B, K)],
            [rows_of(24)], flops=38 * 4 * 2 * 64 * 256 * 128, size=8 << 20,
        )(b1, q1, q2)
        c6, c6_x5, x3, b3c, x4, b4, x5, b5 = call(
            chip_down_kernel, [VMEM] * 5,
            [shape(1, B, K), shape(2, B, K), shape(22, B, K), shape(24, B, K), shape(10, B, K), shape(10, B, K),
             shape(4, B, K), shape(4, B, K)],
            [rows_of(20)], flops=36 * 4 * 2 * 64 * 256 * 128, size=6 << 20,
        )(*around(b3), q_chip)
        operands = ([slab_order] if last else []) + gather(c6, c6_x5)
        operands += [x5, b5, x4, b4, x3, b3c, x2, b2, x1, b1, x0, b0, qc, q_chip, q2, q1, q0]
        operands += [earlier] if last else []
        out_shape = [shape(8, B, K)] * 4 if last else [shape(32, B, K)] * 2 + [shape(11, B, K)] * 2
        return call(
            functools.partial(up_kernel, last),
            ([SMEM] if last else []) + [VMEM] * (len(operands) - last), out_shape,
            [rows_of(34), rows_of(34), rows_of(6), rows_of(34), rows_of(34), rows_of(36), rows_of(34)],
            flops=130 * 4 * 2 * 64 * 256 * 128, size=20 << 20, room=9,
        )(*operands)

    first, load_next, next_in, next_out = cycle(2 * halo, adjoint_load, got_in, got_out)
    load_out = swap_out(next_out)
    load_in = swap_in(next_in)
    parts = cycle(0, load_next, load_in, load_out, first)

    groups = lax.axis_size("grp")
    arrived = [parts[0]]
    for s in range(1, groups):
        arrived.append(lax.ppermute(parts[s], "grp", [(i, (i + s) % groups) for i in range(groups)]))
    return pl.pallas_call(
        place_kernel, name="place", in_specs=[VMEM] * 4, out_specs=ANY, out_shape=shape(32, B, K),
        scratch_shapes=[pltpu.SemaphoreType.DMA((4,))],
        compiler_params=pltpu.CompilerParams(vmem_limit_bytes=4 << 20),
    )(*arrived)


def solution(mesh):
    placed = (
        P(("grp", "dev"), None, None),
        P(None, ("grp", "dev"), None, None),
        P(None, "grp", None, None, None),
        P(("grp", "dev"), None),
    )

    return jax.shard_map(
        shards, mesh=mesh, in_specs=placed, out_specs=P(("grp", "dev"), None, None), check_vma=False
    )
```

```python
import functools

import jax
import jax.numpy as jnp
from jax import lax
from jax.experimental import pallas as pl
from jax.experimental.pallas import tpu as pltpu
from jax.sharding import PartitionSpec as P


F32, BF16 = jnp.float32, jnp.bfloat16
DAMPING = 0.8
B, K = 64, 128
FINE = (32, 16, 8)
HALO = (11, 5, 2)
OWN_AT = (0, 32, 48)
CHIP = (4, 2, 1)
COARSE = (16, 8, 4)
COARSE_AT = (0, 16, 24)


def split_pair(pair, first_ref, second_ref):
    lane = lax.broadcasted_iota(jnp.int32, pair.shape, 1)
    high = pair.astype(BF16).astype(F32)
    low = pair - high
    left = lane < 64
    first_ref[...] = jnp.where(left, high, pltpu.roll(low, 64, 1)).astype(BF16)
    second_ref[...] = jnp.where(left, pltpu.roll(high, 64, 1), low).astype(BF16)


def split_row(smooth_lower, diag_upper, row_ref):
    lane = lax.broadcasted_iota(jnp.int32, smooth_lower.shape, 1)
    smooth_lower = jnp.where(lane < 64, smooth_lower * DAMPING, smooth_lower)
    split_pair(smooth_lower, row_ref.at[0:64], row_ref.at[64:128])
    split_pair(diag_upper, row_ref.at[128:192], row_ref.at[192:256])


def stack_rhs(value):
    high = value.astype(BF16)
    low = (value - high.astype(F32)).astype(BF16)
    return jnp.concatenate([high, high, low, low], axis=0)


def product(blocks, value):
    return jnp.dot(
        jnp.concatenate([blocks, blocks], axis=1), stack_rhs(value), preferred_element_type=F32
    )


def grouped(start, stop, size, body, carry=()):
    groups = (stop - start) // size
    if groups > 1:
        carry = lax.fori_loop(
            0, groups, lambda g, held: body(start + g * size, size, held), carry
        )
        start += groups * size
    while start < stop:
        count = min(size, stop - start)
        carry = body(start, count, carry)
        start += count
    return carry


def smooth(rows, q_ref, q_at, source, store, size=17):
    def body(first, count, carry):
        values = [source(first + u) for u in range(count)]
        outs = [product(q_ref[q_at + first + u, 0:64, :], values[u]) for u in range(count)]
        for u in range(count):
            store(first + u, outs[u], values[u])
        return carry

    grouped(0, rows, size, body)


def sweep(rows, q_ref, q_at, source, emit, size=17):
    def lower(k):
        return q_ref[q_at + k, 64:128, :]

    def diag(k):
        return q_ref[q_at + k, 128:192, :]

    def upper(k):
        return q_ref[q_at + k, 192:256, :]

    below = product(lower(1), source(0))
    out = product(jnp.concatenate([diag(1), lower(2)], axis=0), source(1))
    carry = (below + out[0:64], out[64:128])

    def body(first, count, carry):
        total, below = carry
        values = [source(first + u) for u in range(count)]
        outs = []
        for u in range(count):
            k = first + u
            blocks = jnp.concatenate([upper(k - 1), diag(k), lower(k + 1)], axis=0)
            outs.append(product(blocks, values[u]))
        for u in range(count):
            emit(first + u - 1, total + outs[u][0:64])
            total = outs[u][64:128] + below
            below = outs[u][128:192]
        return total, below

    total, below = grouped(2, rows - 1, size, body, carry)
    emit(rows - 2, total + product(upper(rows - 2), source(rows - 1)))


class Copies:
    def __init__(self, sems):
        self.sems, self.used = sems, 0

    def start(self, source, target):
        copy = pltpu.make_async_copy(source, target, self.sems.at[self.used])
        copy.start()
        self.used += 1
        return copy


def wait_all(copies):
    for copy in copies:
        copy.wait()


ANY = pl.BlockSpec(memory_space=pl.ANY)
SMEM = pl.BlockSpec(memory_space=pltpu.SMEM)
VMEM = pl.BlockSpec(memory_space=pltpu.VMEM)


def shape(*dims, dtype=F32):
    return jax.ShapeDtypeStruct(dims, dtype)


def split_shape(rows):
    return shape(rows, 256, 128, dtype=BF16)


def call(kernel, in_specs, out_shape, scratch=(), flops=0, size=0, room=4, aliases=None):
    return pl.pallas_call(
        kernel,
        in_specs=in_specs,
        out_specs=jax.tree.map(lambda _: VMEM, out_shape),
        out_shape=out_shape,
        scratch_shapes=list(scratch),
        input_output_aliases=aliases or {},
        cost_estimate=pl.CostEstimate(flops=flops, bytes_accessed=size, transcendentals=0),
        compiler_params=pltpu.CompilerParams(vmem_limit_bytes=room << 20),
    )


def rows_of(count):
    return pltpu.VMEM((count, B, K), F32)


def device_parity():
    return lax.rem(lax.axis_index("dev"), 2)


def pack_row(buf, i, target, at):
    target[at] = jnp.concatenate([buf[3, i], buf[0, i]], axis=1)
    target[at + 1] = jnp.concatenate([buf[1, i], buf[2, i]], axis=1)


def send_kernel(outward, ops, load, sent, buf, sems):
    parity = device_parity()
    last = parity if outward else 1 - parity
    copies = Copies(sems)
    halo = HALO[0]
    begin = (FINE[0] - halo) * last
    half = halo // 2
    first = copies.start(ops.at[:, pl.ds(begin, half)], buf.at[:, pl.ds(0, half)])
    second = copies.start(
        ops.at[:, pl.ds(begin + half, halo - half)], buf.at[:, pl.ds(half, halo - half)]
    )
    values = copies.start(load.at[pl.ds(begin, halo)], sent.at[pl.ds(2 * halo, halo)])
    first.wait()
    for i in range(halo):
        if i == half:
            second.wait()
        pack_row(buf, i, sent, 2 * i)
    values.wait()


def send_rest_kernel(ops, to_in, to_out, own, buf, sems):
    parity = device_parity()
    copies = Copies(sems)
    started = []
    for level, at in ((1, 0), (2, 5)):
        rows, halo = FINE[level], HALO[level]
        for side, last in ((0, 1 - parity), (1, parity)):
            begin = OWN_AT[level] + (rows - halo) * last
            target = buf.at[:, pl.ds(7 * side + at, halo)]
            started.append(copies.start(ops.at[:, pl.ds(begin, halo)], target))
    started.append(copies.start(ops.at[:, pl.ds(56, 7)], buf.at[:, pl.ds(14, 7)]))
    wait_all(started)

    def row(i, carry):
        pack_row(buf, i, to_in, 2 * i)
        pack_row(buf, i + 7, to_out, 2 * i)
        pack_row(buf, i + 14, own, 2 * i)
        return carry

    lax.fori_loop(0, 7, row, 0)


COARSE_IN = (1, 19, 29)


def split_rows(source, begin, rows, target, at):
    def pair_of_rows(i, carry):
        for u in range(2):
            k = begin + 2 * i + u
            split_row(
                jnp.concatenate([source[3, k], source[0, k]], axis=1),
                jnp.concatenate([source[1, k], source[2, k]], axis=1),
                target.at[at + 2 * i + u],
            )
        return carry

    lax.fori_loop(0, rows // 2, pair_of_rows, 0)


def own_kernel(ops, q0, q1, q2, buf, sems):
    copies = Copies(sems)
    parts = []
    for begin, rows, target, at in ((0, 16, q0, 11), (16, 16, q0, 27), (32, 16, q1, 5), (48, 8, q2, 2)):
        part = pl.ds(begin, rows)
        parts.append((copies.start(ops.at[:, part], buf.at[:, part]), begin, rows, target, at))
    for load, begin, rows, target, at in parts:
        load.wait()
        split_rows(buf, begin, rows, target, at)


def own_coarse_kernel(coarse, qc):
    for level in range(3):
        split_rows(coarse, COARSE_AT[level], COARSE[level], qc, COARSE_IN[level])


def halo_kernel(levels, got_in, got_out, *refs):
    parity = device_parity()
    targets = refs[len(levels):]
    at = 0
    for level, target in zip(levels, targets):
        rows, halo = FINE[level], HALO[level]
        for got, right in ((got_in, 1 - parity), (got_out, parity)):
            begin = (rows + halo) * right

            def row(i, carry):
                split_row(got[2 * (at + i)], got[2 * (at + i) + 1], target.at[begin + i])
                return carry

            lax.fori_loop(0, halo, row, 0)
        at += halo


CHIP_AT = (0, 4, 6)
CHIPQ_AT = (0, 24, 36)
CHIPQ_ROWS = 42


def chip_slots(parity):
    return (
        (0, 0, 2 + parity),
        (1, 0, 3 - parity),
        (2, 0, 1 + 3 * parity),
        (2, 1, 5 * parity),
        (3, 0, 4 - 3 * parity),
        (3, 1, 5 - 5 * parity),
    )


def chip_send_kernel(own, partner, both):
    near = device_parity()

    def own_row(i, carry):
        both[i] = own[i]
        return carry

    lax.fori_loop(0, 14, own_row, 0)
    for i in range(3):
        for u in range(2):
            both[14 + 2 * i + u] = partner[2 * (near + i) + u]
    for u in range(2):
        both[20 + u] = partner[2 * (CHIP_AT[1] + near) + u]


def chip_kernel(own, partner, mine, theirs, q_chip):
    parity = device_parity()
    arrays = (own, partner, mine, theirs)
    for which, offset, slot in chip_slots(parity):
        if offset:
            near = 1 - parity if which == 2 else parity
            moves = [(14 + 2 * i, 4 * slot + near + i) for i in range(3)]
            moves.append((20, CHIPQ_AT[1] + 2 * slot + near))
        else:
            moves = [
                (2 * (CHIP_AT[level] + i), CHIPQ_AT[level] + slot * CHIP[level] + i)
                for level in range(3)
                for i in range(CHIP[level])
            ]
        for at, target in moves:
            split_row(arrays[which][at], arrays[which][at + 1], q_chip.at[target])


def restrict(r, target, rows, shift):
    def body(first, count, carry):
        for u in range(count):
            i = first + u
            target[i] = 0.5 * (r[2 * i + shift] + r[2 * i + shift + 1])
        return carry

    grouped(0, rows, 4, body)


def residual_into(r, b):
    def emit(k, value):
        r[k - 1] = b[k] - value

    return emit


def down_fine_kernel(at, load, load_in, load_out, q0, x0, b0, b1, r):
    parity = device_parity()
    rows, halo = FINE[0], HALO[0]
    for source, shift, count, begin in (
        (load, 0, rows, halo),
        (load_in, at, halo, (rows + halo) * (1 - parity)),
        (load_out, at, halo, (rows + halo) * parity),
    ):

        def keep(i, value, given):
            x0[begin + i] = value
            b0[begin + i] = given

        smooth(count, q0, begin, lambda i: source[shift + i], keep)
    sweep(54, q0, 0, lambda k: x0[k], residual_into(r, b0))
    restrict(r, b1, 26, 0)


def level_down(rows, q, q_at, b, x, r):
    def keep(i, value, given):
        x[i] = value

    smooth(rows, q, q_at, lambda i: b[i], keep)
    sweep(rows, q, q_at, lambda k: x[k], residual_into(r, b))


def down_kernel(b1, q1, q2, x1, x2, b2, b3, r):
    level_down(26, q1, 0, b1, x1, r)
    restrict(r, b2, 12, 0)
    level_down(12, q2, 0, b2, x2, r)
    restrict(r, b3, 4, 1)


def chip_down_kernel(own, partner, mine, theirs, q, c6, c6_x5, x3, b3, x4, b4, x5, b5, r):
    parity = device_parity()
    arrays = (own, partner, mine, theirs)
    for which, offset, slot in chip_slots(parity):
        for i in range(4):
            b3[4 * slot + i] = arrays[which][4 * offset + i]

    def keep(i, value, given):
        x3[i] = value

    smooth(22, q, 1, lambda i: b3[i + 1], keep)

    def emit(k, value):
        r[k - 1] = b3[k + 1] - value

    sweep(22, q, 1, lambda k: x3[k], emit)
    restrict(r, b4, 10, 0)
    level_down(10, q, CHIPQ_AT[1] + 1, b4, x4, r)
    restrict(r, b5, 4, 0)
    level_down(4, q, CHIPQ_AT[2] + 1, b5, x5, r)
    mean = 0.5 * (r[0] + r[1])
    c6[0] = mean
    c6_x5[0] = mean
    c6_x5[1] = x5[1 + parity]


def row_kernel(own, ahead, across, behind, row, row_x5):
    for i, part in enumerate((own, ahead, across, behind)):
        row[i] = part[0]
        row_x5[i] = part[0]

    @pl.when(device_parity() == 0)
    def _():
        row_x5[4] = ahead[1]

    @pl.when(device_parity() == 1)
    def _():
        row_x5[4] = behind[1]


def up_kernel(last, *refs):
    refs = list(refs)

    def take(count):
        taken = refs[:count]
        del refs[:count]
        return taken

    order = take(1)[0] if last else None
    gathered = take(4)
    x5, b5, x4, b4, x3, b3, x2, b2, x1, b1, x0, b0, qc, qk, q2, q1, q0 = take(17)
    sums = take(1)[0] if last else None
    outs = take(4)
    xc, bc, xk5, f, g, xp, r = refs
    position = lax.axis_index("dev")
    parity, chip = lax.rem(position, 2), lax.div(position, 2)
    row_y, row_x = lax.div(chip, 4), lax.rem(chip, 4)

    for sy in range(4):
        for sx in range(4):
            place = 4 * lax.rem(row_y + 4 - sy, 4) + lax.rem(row_x + 4 - sx, 4)
            bc[1 + place] = gathered[sy][sx]
    zero = jnp.zeros((B, K), F32)
    for level in range(3):
        for edge in (COARSE_IN[level] - 1, COARSE_IN[level] + COARSE[level]):
            xc[edge] = zero

    for level in range(3):
        rows, base = COARSE[level], COARSE_IN[level]

        def keep(i, value, given):
            xc[base + i] = value

        smooth(rows, qc, base, lambda i: bc[base + i], keep)
        if level == 2:
            break

        def emit(k, value):
            r[k - 1] = bc[base - 1 + k] - value

        sweep(rows + 2, qc, base - 1, lambda k: xc[base - 1 + k], emit)
        following = COARSE_IN[level + 1]
        for i in range(rows // 2):
            bc[following + i] = 0.5 * (r[2 * i] + r[2 * i + 1])

    for level in (2, 1, 0):
        rows, base = COARSE[level], COARSE_IN[level]
        if level < 2:
            below = COARSE_IN[level + 1]
            for i in range(rows):
                xc[base + i] = xc[base + i] + xc[below + i // 2]

        def emit(k, value):
            r[k - 1] = bc[base - 1 + k] - value

        sweep(rows + 2, qc, base - 1, lambda k: xc[base - 1 + k], emit)

        def keep(i, value, given):
            xc[base + i] = xc[base + i] + value

        smooth(rows, qc, base, lambda i: r[i], keep)

    def post(rows, q, q_at, right_side, b_at, target):
        def emit(k, value):
            r[k - 1] = right_side[b_at + k - 1] - value

        sweep(rows + 4, q, q_at, lambda k: xp[k], emit)

        def keep(i, value, given):
            target[i] = xp[i + 1] + value

        smooth(rows + 2, q, q_at + 1, lambda i: r[i], keep)

    def correct(rows, values, x_at, source):
        def body(first, count, carry):
            for u in range(count):
                j = first + u
                value = source[j]
                xp[2 * j] = values[x_at + 2 * j] + value
                xp[2 * j + 1] = values[x_at + 2 * j + 1] + value
            return carry

        grouped(0, rows // 2 + 2, 3, body)

    for i in range(4):
        xk5[1 + i] = x5[i]
    inside = row_x != 3 * parity
    outermost = chip == 15 * parity

    @pl.when(inside)
    def _():
        xk5[5 * parity] = gathered[0][4]

    @pl.when(jnp.logical_not(inside) & (parity == 0))
    def _():
        xk5[0] = gathered[1][4]

    @pl.when(jnp.logical_not(inside) & (parity == 1))
    def _():
        xk5[5] = gathered[3][4]

    @pl.when(outermost)
    def _():
        xk5[5 * parity] = zero

    for k in range(5):
        xp[k] = xk5[k + parity] + xc[chip + lax.div(k + parity, 2)]
    post(1, qk, CHIPQ_AT[2] + parity, b5, parity, f)
    correct(2, x4, 1 + 2 * parity, f)
    post(2, qk, CHIPQ_AT[1] + 2 + 2 * parity, b4, 2 + 2 * parity, g)
    correct(4, x3, 5 + 4 * parity, g)
    post(4, qk, 6 + 4 * parity, b3, 7 + 4 * parity, f)
    correct(8, x2, 0, f)
    post(8, q2, 0, b2, 1, g)
    correct(16, x1, 3, g)
    post(16, q1, 3, b1, 4, f)
    correct(32, x0, 9, f)
    post(32, q0, 9, b0, 10, g)

    if last:
        group = lax.axis_index("grp")
        for s in range(4):
            base = 8 * lax.rem(group + s, 4)
            for u in range(8):
                pick = order[0, base + u]
                outs[s][u] = sums[pick] + g[pick + 1]
        return
    first_out, load_next, next_in, next_out = outs

    def emit(k, value):
        load_next[k - 1] = b0[k + 10] - value
        first_out[k - 1] = g[k]

    sweep(34, q0, 10, lambda k: g[k], emit)

    def edge_row(i, carry):
        next_in[i] = load_next[21 * (1 - parity) + i]
        next_out[i] = load_next[21 * parity + i]
        return carry

    lax.fori_loop(0, 11, edge_row, 0)


def place_kernel(part0, part1, part2, part3, out, sems):
    copies = Copies(sems)
    started = []
    group = lax.axis_index("grp")
    for s, part in enumerate((part0, part1, part2, part3)):
        begin = 8 * lax.rem(group + 4 - s, 4)
        started.append(copies.start(part, out.at[pl.ds(begin, 8)]))
    wait_all(started)


def shards(adjoint_load, local_ops, coarse_ops, slab_order):
    devices = lax.axis_size("dev")
    side = 4

    def swap_in(value):
        return lax.ppermute(value, "dev", [(i, i ^ 1) for i in range(devices)])

    def swap_out(value):
        route = []
        for i in range(1, devices - 1, 2):
            route += [(i, i + 1), (i + 1, i)]
        return lax.ppermute(value, "dev", route)

    def around(value):
        partner = swap_in(value)
        both = jnp.concatenate([value, partner], axis=0)
        mine = swap_out(both)
        theirs = swap_in(mine)
        return value, partner, mine, theirs

    def shift(value, along_y, step):
        route = []
        for i in range(devices):
            y, x, core = i // (2 * side), i // 2 % side, i % 2
            if along_y:
                y = (y + step) % side
            else:
                x = (x + step) % side
            route.append((i, (y * side + x) * 2 + core))
        return lax.ppermute(value, "dev", route)

    def gather(c6, c6_x5):
        across = shift(c6, False, 2)
        parts = (c6_x5, shift(c6_x5, False, 1), across, shift(c6_x5, False, 3))
        row, row_x5 = call(
            row_kernel, [VMEM] * 4, [shape(4, B, K), shape(5, B, K)], size=1 << 18
        )(*parts)
        across = shift(row, True, 2)
        return [row_x5, shift(row_x5, True, 1), across, shift(row_x5, True, 3)]

    halo = HALO[0]

    def send(outward):
        return call(
            functools.partial(send_kernel, outward), [ANY, ANY], shape(3 * halo, B, K),
            [pltpu.VMEM((4, halo, B, B), F32), pltpu.SemaphoreType.DMA((3,))], size=4 << 20, room=58,
        )(local_ops, adjoint_load)

    to_out = send(True)
    got_out = swap_out(to_out)
    to_in = send(False)
    got_in = swap_in(to_in)
    rest_in, rest_out, own7 = call(
        send_rest_kernel, [ANY], [shape(14, B, K)] * 3,
        [pltpu.VMEM((4, 21, B, B), F32), pltpu.SemaphoreType.DMA((5,))], size=4 << 20, room=50,
    )(local_ops)
    more_out = swap_out(rest_out)
    more_in = swap_in(rest_in)
    q0, q1, q2 = call(
        own_kernel, [ANY], [split_shape(54), split_shape(26), split_shape(12)],
        [pltpu.VMEM((4, 56, B, B), F32), pltpu.SemaphoreType.DMA((4,))], size=8 << 20, room=40,
    )(local_ops)
    qc = call(own_coarse_kernel, [VMEM], split_shape(34), size=6 << 20)(coarse_ops[:, 0])
    q0 = call(
        functools.partial(halo_kernel, (0,)), [VMEM] * 3, [split_shape(54)],
        size=4 << 20, aliases={2: 0},
    )(got_in, got_out, q0)[0]
    q1, q2 = call(
        functools.partial(halo_kernel, (1, 2)), [VMEM] * 4, [split_shape(26), split_shape(12)],
        size=4 << 20, aliases={2: 0, 3: 1},
    )(more_in, more_out, q1, q2)
    partner7 = swap_in(own7)
    both = call(chip_send_kernel, [VMEM] * 2, shape(22, B, K), size=2 << 20)(own7, partner7)
    both = lax.optimization_barrier((both, q0))[0]
    mine = swap_out(both)
    theirs = swap_in(mine)
    q_chip = call(
        chip_kernel, [VMEM] * 4, split_shape(CHIPQ_ROWS), size=6 << 20,
    )(own7, partner7, mine, theirs)

    def cycle(at, load, load_in, load_out, earlier=None):
        last = earlier is not None
        x0, b0, b1 = call(
            functools.partial(down_fine_kernel, at),
            [VMEM] * 4, [shape(54, B, K), shape(54, B, K), shape(26, B, K)],
            [rows_of(52)], flops=54 * 4 * 2 * 64 * 256 * 128, size=16 << 20,
        )(load, load_in, load_out, q0)
        x1, x2, b2, b3 = call(
            down_kernel,
            [VMEM] * 3, [shape(26, B, K), shape(12, B, K), shape(12, B, K), shape(4, B, K)],
            [rows_of(24)], flops=38 * 4 * 2 * 64 * 256 * 128, size=8 << 20,
        )(b1, q1, q2)
        c6, c6_x5, x3, b3c, x4, b4, x5, b5 = call(
            chip_down_kernel, [VMEM] * 5,
            [shape(1, B, K), shape(2, B, K), shape(22, B, K), shape(24, B, K), shape(10, B, K), shape(10, B, K),
             shape(4, B, K), shape(4, B, K)],
            [rows_of(20)], flops=36 * 4 * 2 * 64 * 256 * 128, size=6 << 20,
        )(*around(b3), q_chip)
        operands = ([slab_order] if last else []) + gather(c6, c6_x5)
        operands += [x5, b5, x4, b4, x3, b3c, x2, b2, x1, b1, x0, b0, qc, q_chip, q2, q1, q0]
        operands += [earlier] if last else []
        out_shape = [shape(8, B, K)] * 4 if last else [shape(32, B, K)] * 2 + [shape(11, B, K)] * 2
        return call(
            functools.partial(up_kernel, last),
            ([SMEM] if last else []) + [VMEM] * (len(operands) - last), out_shape,
            [rows_of(34), rows_of(34), rows_of(6), rows_of(34), rows_of(34), rows_of(36), rows_of(34)],
            flops=130 * 4 * 2 * 64 * 256 * 128, size=20 << 20, room=9,
        )(*operands)

    first, load_next, next_in, next_out = cycle(2 * halo, adjoint_load, got_in, got_out)
    load_out = swap_out(next_out)
    load_in = swap_in(next_in)
    parts = cycle(0, load_next, load_in, load_out, first)

    groups = lax.axis_size("grp")
    arrived = [parts[0]]
    for s in range(1, groups):
        arrived.append(lax.ppermute(parts[s], "grp", [(i, (i + s) % groups) for i in range(groups)]))
    return pl.pallas_call(
        place_kernel, name="place", in_specs=[VMEM] * 4, out_specs=ANY, out_shape=shape(32, B, K),
        scratch_shapes=[pltpu.SemaphoreType.DMA((4,))],
        compiler_params=pltpu.CompilerParams(vmem_limit_bytes=4 << 20),
    )(*arrived)


def solution(mesh):
    placed = (
        P(("grp", "dev"), None, None),
        P(None, ("grp", "dev"), None, None),
        P(None, "grp", None, None, None),
        P(("grp", "dev"), None),
    )

    return jax.shard_map(
        shards, mesh=mesh, in_specs=placed, out_specs=P(("grp", "dev"), None, None), check_vma=False
    )
```
